32 devices in a mesh: dp: 16 (over z, y, x), tensor: 2 (over core).
Axes of the slice: x: 2, y: 2, z: 4, core: 2. Of those that a mesh axis runs over, the one named last changes fastest.
Arguments:
- block_input: float32 [16, 1024, 1536], P('dp', 'tensor'), may hold values from -6 to 6
- cotangent: float32 [16, 1024, 1536], P('dp', 'tensor'), may hold values from -6 to 6
- segments: int32 [16, 1024], P('dp'), may hold values from 0 to 2, never falling along the last dimension, each value on 1 to 512 neighbouring positions
- weight_zx: float32 [1536, 2, 3072], P('dp', None, 'tensor'), may hold values from -0.15625 to 0.15625
- weight_bc: float32 [1536, 256], P(('dp', 'tensor')), may hold values from -0.15625 to 0.15625
- weight_dt: float32 [1536, 48], P('dp', 'tensor'), may hold values from -0.15625 to 0.15625
- weight_out: float32 [3072, 1536], P('tensor', 'dp'), may hold values from -0.109375 to 0.109375
- input_gain: float32 [1536], replicated, may hold values from 0.1 to 1.9
- gate_gain: float32 [3072], replicated, may hold values from 0.1 to 1.9
- conv_taps: float32 [4, 3328], replicated, may hold values from -3 to 3
- conv_bias: float32 [3328], replicated, may hold values from -0.5 to 0.5
- dt_bias: float32 [48], replicated, may hold values from -7 to -2.3
- a_log: float32 [48], replicated, may hold values from 0 to 2.77
- d_skip: float32 [48], replicated, may hold values from 0.5 to 2
- first_zx: float32 [1536, 2, 3072], P('dp', None, 'tensor'), may hold values from -24 to 24
- first_bc: float32 [1536, 256], P(('dp', 'tensor')), may hold values from -24 to 24
- first_dt: float32 [1536, 48], P('dp', 'tensor'), may hold values from -24 to 24
- first_out: float32 [3072, 1536], P('tensor', 'dp'), may hold values from -80 to 80
- first_ingain: float32 [1536], replicated, may hold values from -80 to 80
- first_gategain: float32 [3072], replicated, may hold values from -80 to 80
- first_taps: float32 [4, 3328], replicated, may hold values from -80 to 80
- first_convbias: float32 [3328], replicated, may hold values from -80 to 80
- first_dtbias: float32 [48], replicated, may hold values from -224 to 224
- first_alog: float32 [48], replicated, may hold values from -224 to 224
- first_dskip: float32 [48], replicated, may hold values from -224 to 224
- second_zx: float32 [1536, 2, 3072], P('dp', None, 'tensor'), may hold values from 29.4912 to 294.912
- second_bc: float32 [1536, 256], P(('dp', 'tensor')), may hold values from 29.4912 to 294.912
- second_dt: float32 [1536, 48], P('dp', 'tensor'), may hold values from 29.4912 to 294.912
- second_out: float32 [3072, 1536], P('tensor', 'dp'), may hold values from 327.68 to 3276.8
- second_ingain: float32 [1536], replicated, may hold values from 327.68 to 3276.8
- second_gategain: float32 [3072], replicated, may hold values from 327.68 to 3276.8
- second_taps: float32 [4, 3328], replicated, may hold values from 327.68 to 3276.8
- second_convbias: float32 [3328], replicated, may hold values from 327.68 to 3276.8
- second_dtbias: float32 [48], replicated, may hold values from 2949.12 to 29491.2
- second_alog: float32 [48], replicated, may hold values from 2949.12 to 29491.2
- second_dskip: float32 [48], replicated, may hold values from 2949.12 to 29491.2
Outputs:
- block_output: float32 [16, 1024, 1536], P('dp', 'tensor')
- input_grad: float32 [16, 1024, 1536], P('dp', 'tensor')
- grad_zx: float32 [1536, 2, 3072], P('dp', None, 'tensor')
- grad_bc: float32 [1536, 256], P(('dp', 'tensor'))
- grad_dt: float32 [1536, 48], P('dp', 'tensor')
- grad_out: float32 [3072, 1536], P('tensor', 'dp')
- grad_ingain: float32 [1536], replicated
- grad_gategain: float32 [3072], replicated
- grad_taps: float32 [4, 3328], replicated
- grad_convbias: float32 [3328], replicated
- grad_dtbias: float32 [48], replicated
- grad_alog: float32 [48], replicated
- grad_dskip: float32 [48], replicated
- new_zx: float32 [1536, 2, 3072], P('dp', None, 'tensor')
- new_bc: float32 [1536, 256], P(('dp', 'tensor'))
- new_dt: float32 [1536, 48], P('dp', 'tensor')
- new_out: float32 [3072, 1536], P('tensor', 'dp')
- new_ingain: float32 [1536], replicated
- new_gategain: float32 [3072], replicated
- new_taps: float32 [4, 3328], replicated
- new_convbias: float32 [3328], replicated
- new_dtbias: float32 [48], replicated
- new_alog: float32 [48], replicated
- new_dskip: float32 [48], replicated
- new_first_zx: float32 [1536, 2, 3072], P('dp', None, 'tensor')
- new_first_bc: float32 [1536, 256], P(('dp', 'tensor'))
- new_first_dt: float32 [1536, 48], P('dp', 'tensor')
- new_first_out: float32 [3072, 1536], P('tensor', 'dp')
- new_first_ingain: float32 [1536], replicated
- new_first_gategain: float32 [3072], replicated
- new_first_taps: float32 [4, 3328], replicated
- new_first_convbias: float32 [3328], replicated
- new_first_dtbias: float32 [48], replicated
- new_first_alog: float32 [48], replicated
- new_first_dskip: float32 [48], replicated
- new_second_zx: float32 [1536, 2, 3072], P('dp', None, 'tensor')
- new_second_bc: float32 [1536, 256], P(('dp', 'tensor'))
- new_second_dt: float32 [1536, 48], P('dp', 'tensor')
- new_second_out: float32 [3072, 1536], P('tensor', 'dp')
- new_second_ingain: float32 [1536], replicated
- new_second_gategain: float32 [3072], replicated
- new_second_taps: float32 [4, 3328], replicated
- new_second_convbias: float32 [3328], replicated
- new_second_dtbias: float32 [48], replicated
- new_second_alog: float32 [48], replicated
- new_second_dskip: float32 [48], replicated
The draws below stay inside these ranges and needn't reach their ends.
Inputs may be any that keep to these rules, and one draw needn't show every extreme that they name: `segments`: along each sequence the document numbers never fall; each document has 1 to 512 consecutive tokens.
All inputs are finite; a program needn't handle non-finite values.
Results may differ from the reference program's by a relative error of at most 0.0093.
The reference program's roundings to bfloat16 on the way count: a program that leaves them out, or rounds other values in their place, can miss the bound.
Values may be sent and summed in bfloat16 or wider, within the bound.
No kernel may reach another device: no remote copies, remote signals or barrier semaphores. Data moves between devices by JAX's collectives and lax.ppermute only.
A program may use at most 384 MiB of HBM per device.

```python
import math
import jax
import jax.numpy as jnp
import numpy as np
from jax import lax

D = 1536
INNER = 3072
HEADS = 48
STATE = 128
CONV = 4
SPAN = 256
LEN = 1024
STEP = 3
SEQS = 16
CONVCH = 3328
N_TENSOR = 2


def level_of(stream_key, extent, shards, smallest, largest):
    def one(axis_at, shards_of):
        heights = jax.random.uniform(jax.random.fold_in(jax.random.fold_in(stream_key, 6), axis_at), (shards_of,), jnp.float32, smallest / len(shards), largest / len(shards))
        return jnp.repeat(jnp.exp(heights), extent[axis_at] // shards_of).reshape((-1,) + (1,) * (len(extent) - axis_at - 1))

    level = one(*shards[0])
    for cut in shards[1:]:
        level = level * one(*cut)
    return level


def split_up(amount, total, reach, lean):
    loads = [(1 << 20) // math.isqrt(grade ** lean) + 1 for grade in range(2, amount + 1)]
    surplus, given = total - reach - (amount - 1), [1] * (amount - 1)
    while surplus > 0:
        free = [i for i in range(amount - 1) if given[i] < reach]
        mass, left = sum([loads[i] for i in free]), surplus
        for i in free:
            extra = min(reach - given[i], max(1, left * loads[i] // mass), surplus)
            given[i] = given[i] + extra
            surplus = surplus - extra
    return np.array([reach] + given)


def uneven_parts(own_key, number_of, total, limit, skew):
    if number_of == 2:
        one = jax.random.randint(own_key, (), max(1, total - limit), min(limit, total - 1) + 1)
        return jnp.stack([one, total - one])
    lengths = jnp.asarray(split_up(number_of, total, limit, skew), jnp.int32)
    couples = (number_of - 1) // 2
    source_of, taker = lengths[1:1 + 2 * couples:2], lengths[2:2 + 2 * couples:2]
    room = jnp.minimum(source_of - 1, limit - taker)
    moved = jax.random.randint(jax.random.fold_in(own_key, 1), (couples,), 0, 1 << 20) % (room + 1)
    lengths = lengths.at[1:1 + 2 * couples:2].set(source_of - moved).at[2:2 + 2 * couples:2].set(taker + moved)
    return lengths[jax.random.permutation(jax.random.fold_in(own_key, 2), number_of)]


def bell_draw(stream_key, shape, spread, reach, cuts=(), kind=jnp.bfloat16):
    result = jax.random.normal(stream_key, shape, jnp.float32) * spread
    if len(cuts) > 0:
        result = level_of(stream_key, shape, cuts, -0.22, 0.18) * result
    return jnp.clip(result, min=-reach, max=reach).astype(kind)


def setup_inputs(seed: int = 0) -> dict:
    arg_keys = jax.random.split(jax.random.key(seed), 37)
    block_input = bell_draw(arg_keys[0], (SEQS, LEN, D), 1.0, 6.0, ((0, 16), (1, 2)), jnp.float32)
    cotangent = bell_draw(arg_keys[1], (SEQS, LEN, D), 1.0, 6.0, ((0, 16), (1, 2)), jnp.float32)
    segments = jax.vmap(lambda own: jnp.searchsorted(jnp.cumsum(uneven_parts(own, 3, LEN, LEN // 2, 1)), jnp.arange(LEN), side="right"))(jax.random.split(arg_keys[2], SEQS)).reshape((SEQS, LEN)).astype(jnp.int32)
    weight_zx = bell_draw(arg_keys[3], (D, 2, INNER), D ** -0.5, 0.15625, ((0, 16), (2, 2)), jnp.float32)
    weight_bc = bell_draw(arg_keys[4], (D, 2 * STATE), D ** -0.5, 0.15625, ((0, 32),), jnp.float32)
    weight_dt = bell_draw(arg_keys[5], (D, HEADS), D ** -0.5, 0.15625, ((0, 16), (1, 2)), jnp.float32)
    weight_out = bell_draw(arg_keys[6], (INNER, D), INNER ** -0.5, 0.109375, ((0, 2), (1, 16)), jnp.float32)
    input_gain = jnp.clip(1.0 + 0.18 * jax.random.normal(arg_keys[7], (D,), jnp.float32), 0.1, 1.9)
    gate_gain = jnp.clip(1.0 + 0.18 * jax.random.normal(arg_keys[8], (INNER,), jnp.float32), 0.1, 1.9)
    conv_taps = bell_draw(arg_keys[9], (CONV, CONVCH), CONV ** -0.5, 3.0, (), jnp.float32)
    conv_bias = jnp.clip(jax.random.uniform(arg_keys[10], (CONVCH,), jnp.float32, -0.5, 0.5), -0.5, 0.5)
    dt_bias = jnp.clip(jax.random.uniform(arg_keys[11], (HEADS,), jnp.float32, -7.0, -2.3), -7.0, -2.3)
    a_log = jnp.clip(jax.random.uniform(arg_keys[12], (HEADS,), jnp.float32, 0.0, 2.77), 0.0, 2.77)
    d_skip = jnp.clip(jax.random.uniform(arg_keys[13], (HEADS,), jnp.float32, 0.5, 2.0), 0.5, 2.0)
    first_zx = bell_draw(arg_keys[14], (D, 2, INNER), (0.03 * (SEQS * LEN) ** 0.5), 24.0, ((0, 16), (2, 2)), jnp.float32)
    first_bc = bell_draw(arg_keys[15], (D, 2 * STATE), (0.03 * (SEQS * LEN) ** 0.5), 24.0, ((0, 32),), jnp.float32)
    first_dt = bell_draw(arg_keys[16], (D, HEADS), (0.03 * (SEQS * LEN) ** 0.5), 24.0, ((0, 16), (1, 2)), jnp.float32)
    first_out = bell_draw(arg_keys[17], (INNER, D), (0.1 * (SEQS * LEN) ** 0.5), 80.0, ((0, 2), (1, 16)), jnp.float32)
    first_ingain = bell_draw(arg_keys[18], (D,), (0.1 * (SEQS * LEN) ** 0.5), 80.0, (), jnp.float32)
    first_gategain = bell_draw(arg_keys[19], (INNER,), (0.1 * (SEQS * LEN) ** 0.5), 80.0, (), jnp.float32)
    first_taps = bell_draw(arg_keys[20], (CONV, CONVCH), (0.1 * (SEQS * LEN) ** 0.5), 80.0, (), jnp.float32)
    first_convbias = bell_draw(arg_keys[21], (CONVCH,), (0.1 * (SEQS * LEN) ** 0.5), 80.0, (), jnp.float32)
    first_dtbias = bell_draw(arg_keys[22], (HEADS,), (0.3 * (SEQS * LEN) ** 0.5), 224.0, (), jnp.float32)
    first_alog = bell_draw(arg_keys[23], (HEADS,), (0.3 * (SEQS * LEN) ** 0.5), 224.0, (), jnp.float32)
    first_dskip = bell_draw(arg_keys[24], (HEADS,), (0.3 * (SEQS * LEN) ** 0.5), 224.0, (), jnp.float32)
    second_zx = jnp.clip(jnp.exp(math.log(294.912) - 2.3025851 * jax.random.uniform(arg_keys[25], (D, 2, INNER), jnp.float32) ** level_of(arg_keys[25], (D, 2, INNER), ((0, 16), (2, 2)), -0.2, 0.2)), 29.4912, 294.912)
    second_bc = jnp.clip(jnp.exp(math.log(294.912) - 2.3025851 * jax.random.uniform(arg_keys[26], (D, 2 * STATE), jnp.float32) ** level_of(arg_keys[26], (D, 2 * STATE), ((0, 32),), -0.2, 0.2)), 29.4912, 294.912)
    second_dt = jnp.clip(jnp.exp(math.log(294.912) - 2.3025851 * jax.random.uniform(arg_keys[27], (D, HEADS), jnp.float32) ** level_of(arg_keys[27], (D, HEADS), ((0, 16), (1, 2)), -0.2, 0.2)), 29.4912, 294.912)
    second_out = jnp.clip(jnp.exp(math.log(3276.8) - 2.3025851 * jax.random.uniform(arg_keys[28], (INNER, D), jnp.float32) ** level_of(arg_keys[28], (INNER, D), ((0, 2), (1, 16)), -0.2, 0.2)), 327.68, 3276.8)
    second_ingain = jnp.clip(jnp.exp(jax.random.uniform(arg_keys[29], (D,), jnp.float32, math.log(327.68), math.log(3276.8))), 327.68, 3276.8)
    second_gategain = jnp.clip(jnp.exp(jax.random.uniform(arg_keys[30], (INNER,), jnp.float32, math.log(327.68), math.log(3276.8))), 327.68, 3276.8)
    second_taps = jnp.clip(jnp.exp(jax.random.uniform(arg_keys[31], (CONV, CONVCH), jnp.float32, math.log(327.68), math.log(3276.8))), 327.68, 3276.8)
    second_convbias = jnp.clip(jnp.exp(jax.random.uniform(arg_keys[32], (CONVCH,), jnp.float32, math.log(327.68), math.log(3276.8))), 327.68, 3276.8)
    second_dtbias = jnp.clip(jnp.exp(jax.random.uniform(arg_keys[33], (HEADS,), jnp.float32, math.log(2949.12), math.log(29491.2))), 2949.12, 29491.2)
    second_alog = jnp.clip(jnp.exp(jax.random.uniform(arg_keys[34], (HEADS,), jnp.float32, math.log(2949.12), math.log(29491.2))), 2949.12, 29491.2)
    second_dskip = jnp.clip(jnp.exp(jax.random.uniform(arg_keys[35], (HEADS,), jnp.float32, math.log(2949.12), math.log(29491.2))), 2949.12, 29491.2)
    return {"block_input": block_input, "cotangent": cotangent, "segments": segments, "weight_zx": weight_zx, "weight_bc": weight_bc, "weight_dt": weight_dt, "weight_out": weight_out, "input_gain": input_gain, "gate_gain": gate_gain, "conv_taps": conv_taps, "conv_bias": conv_bias, "dt_bias": dt_bias, "a_log": a_log, "d_skip": d_skip, "first_zx": first_zx, "first_bc": first_bc, "first_dt": first_dt, "first_out": first_out, "first_ingain": first_ingain, "first_gategain": first_gategain, "first_taps": first_taps, "first_convbias": first_convbias, "first_dtbias": first_dtbias, "first_alog": first_alog, "first_dskip": first_dskip, "second_zx": second_zx, "second_bc": second_bc, "second_dt": second_dt, "second_out": second_out, "second_ingain": second_ingain, "second_gategain": second_gategain, "second_taps": second_taps, "second_convbias": second_convbias, "second_dtbias": second_dtbias, "second_alog": second_alog, "second_dskip": second_dskip}


norm_eps = 1e-05
learn_rate = 0.01
beta_one = 0.9
beta_two = 0.95
adam_eps = 1e-08
weight_decay = 0.1
highest = lax.Precision.HIGHEST

def mixer_core(gate_input_projection, bc_projection, delta_projection, conv_w, conv_b, dt_bias, a_log, d_skip, seg_ids):
    length = gate_input_projection.shape[0]
    inner_width = gate_input_projection.shape[2]
    head_count = dt_bias.shape[0]
    head_size = inner_width // head_count
    state_size = bc_projection.shape[1] // 2
    block_len = SPAN
    block_count = length // block_len
    gate_part = gate_input_projection[:, 0, :]
    inner_part = gate_input_projection[:, 1, :]
    conv_in = jnp.concatenate([inner_part, bc_projection], axis=1)
    tap_count = conv_w.shape[0]
    mixed_sum = conv_b[None, :] + conv_w[tap_count - 1][None, :] * conv_in
    for offset in range(1, tap_count):
        shifted = jnp.pad(conv_in, ((offset, 0), (0, 0)))[:length]
        earlier = jnp.pad(seg_ids, (offset, 0), constant_values=-1)[:length]
        keep_mask = (earlier == seg_ids).astype(jnp.float32)
        mixed_sum = mixed_sum + conv_w[tap_count - 1 - offset][None, :] * shifted * keep_mask[:, None]
    active = jax.nn.silu(mixed_sum)
    values = active[:, :inner_width].reshape(block_count, block_len, head_count, head_size)
    b_mat = active[:, inner_width:inner_width + state_size].reshape(block_count, block_len, state_size)
    c_mat = active[:, inner_width + state_size:].reshape(block_count, block_len, state_size)
    step_size = jax.nn.softplus(delta_projection + dt_bias[None, :])
    decay_rates = -jnp.exp(a_log)
    log_decay = jnp.transpose((step_size * decay_rates[None, :]).reshape(block_count, block_len, head_count), (0, 2, 1))
    cumulative = jnp.cumsum(log_decay, axis=2)
    block_segs = seg_ids.reshape(block_count, block_len)
    position = jnp.arange(block_len)
    causal = position[:, None] >= position[None, :]
    same_doc = (block_segs[:, :, None] == block_segs[:, None, :]) & causal[None]
    log_gaps = cumulative[:, :, :, None] - cumulative[:, :, None, :]
    decay_table = jnp.where(same_doc[:, None], jnp.exp(jnp.minimum(log_gaps, 0.0)), 0.0)
    scores = jnp.einsum('cin,cjn->cij', c_mat, b_mat, precision=highest)
    weighted = decay_table * scores[:, None]
    scaled = values * step_size.reshape(block_count, block_len, head_count)[..., None]
    intra_part = jnp.einsum('chij,cjhp->cihp', weighted, scaled, precision=highest)
    last_seg = block_segs[:, -1]
    end_mask = (block_segs == last_seg[:, None]).astype(jnp.float32)
    to_end = jnp.exp(cumulative[:, :, -1:] - cumulative) * end_mask[:, None, :]
    states = jnp.einsum('cjn,chj,cjhp->chnp', b_mat, to_end, scaled, precision=highest)
    prev_seg = jnp.concatenate([jnp.full((1,), -1, dtype=jnp.int32), last_seg[:-1].astype(jnp.int32)])
    carry_keep = (last_seg == prev_seg).astype(jnp.float32)[:, None] * jnp.exp(cumulative[:, :, -1])

    def advance(held_state, inputs):
        keep_c, state_c = inputs
        return (keep_c[:, None, None] * held_state + state_c, held_state)
    start_state = jnp.zeros((head_count, state_size, head_size), jnp.float32)
    _, entering = lax.scan(advance, start_state, (carry_keep, states))
    start_mask = (block_segs == prev_seg[:, None]).astype(jnp.float32)
    from_start = jnp.exp(cumulative) * start_mask[:, None, :]
    inter_part = jnp.einsum('cin,chi,chnp->cihp', c_mat, from_start, entering, precision=highest)
    output = intra_part + inter_part + d_skip[None, None, :, None] * values
    return output.reshape(length, inner_width) * jax.nn.silu(gate_part)

def adamw_step(weight, grad, first, second, decayed):
    new_first = beta_one * first + (1.0 - beta_one) * grad
    new_second = beta_two * second + (1.0 - beta_two) * grad * grad
    first_corr = 1.0 - beta_one ** STEP
    second_corr = 1.0 - beta_two ** STEP
    update = new_first / first_corr / (jnp.sqrt(new_second / second_corr) + adam_eps)
    if decayed:
        update = update + weight_decay * weight
    return (weight - learn_rate * update, new_first, new_second)

def reference(block_input, cotangent, segments, weight_zx, weight_bc, weight_dt, weight_out, input_gain, gate_gain, conv_taps, conv_bias, dt_bias, a_log, d_skip, first_zx, first_bc, first_dt, first_out, first_ingain, first_gategain, first_taps, first_convbias, first_dtbias, first_alog, first_dskip, second_zx, second_bc, second_dt, second_out, second_ingain, second_gategain, second_taps, second_convbias, second_dtbias, second_alog, second_dskip):
    groups = N_TENSOR
    head_width = INNER // groups
    group_heads = HEADS // groups
    zx_half = weight_zx.astype(jnp.bfloat16).reshape(D, 2 * INNER)
    bc_half = weight_bc.astype(jnp.bfloat16)
    dt_half = weight_dt.astype(jnp.bfloat16)
    out_half = weight_out.astype(jnp.bfloat16)

    def one_sequence(totals, items):
        rows, cot_rows, seg_ids = items
        inv_in = lax.rsqrt(lax.optimization_barrier(jnp.mean(rows * rows, axis=1, keepdims=True)) + norm_eps)
        normed = (rows * inv_in * input_gain[None, :]).astype(jnp.bfloat16)
        gate_input_projection = jnp.dot(normed, zx_half, preferred_element_type=jnp.float32).reshape(LEN, 2, INNER)
        bc_projection = jnp.dot(normed, bc_half, preferred_element_type=jnp.float32)
        delta_projection = jnp.dot(normed, dt_half, preferred_element_type=jnp.float32)

        def local_mix(part_zx, part_bc, part_dt, taps, bias, dtb, alog, dskip):
            return mixer_core(part_zx, part_bc, part_dt, taps, bias, dtb, alog, dskip, seg_ids)
        gated_parts = []
        pullbacks = []
        for group_idx in range(groups):
            col_lo = group_idx * head_width
            head_lo = group_idx * group_heads
            taps_group = jnp.concatenate([conv_taps[:, col_lo:col_lo + head_width], conv_taps[:, INNER:]], axis=1)
            bias_group = jnp.concatenate([conv_bias[col_lo:col_lo + head_width], conv_bias[INNER:]], axis=0)
            gated_group, pullback = jax.vjp(local_mix, gate_input_projection[:, :, col_lo:col_lo + head_width], bc_projection, delta_projection[:, head_lo:head_lo + group_heads], taps_group, bias_group, dt_bias[head_lo:head_lo + group_heads], a_log[head_lo:head_lo + group_heads], d_skip[head_lo:head_lo + group_heads])
            gated_parts.append(gated_group)
            pullbacks.append(pullback)
        gated = jnp.concatenate(gated_parts, axis=1)
        inv_gate = lax.rsqrt(lax.optimization_barrier(jnp.mean(gated * gated, axis=1, keepdims=True)) + norm_eps)
        gate_normalized = (gated * inv_gate * gate_gain[None, :]).astype(jnp.bfloat16)
        out_rows = rows + jnp.dot(gate_normalized, out_half, preferred_element_type=jnp.float32)
        cot_half = cot_rows.astype(jnp.bfloat16)
        grad_out = jnp.dot(gate_normalized.T, cot_half, preferred_element_type=jnp.float32)
        gate_gradient = jnp.dot(cot_half, out_half.T, preferred_element_type=jnp.float32)
        grad_gategain = lax.optimization_barrier(jnp.sum(gate_gradient * gated * inv_gate, axis=0))
        cross_sum = lax.optimization_barrier(jnp.sum(gate_gradient * gate_gain[None, :] * gated, axis=1, keepdims=True))
        d_gated = inv_gate * gate_gain[None, :] * gate_gradient - gated * inv_gate ** 3 * cross_sum / INNER
        zx_parts = []
        dt_parts = []
        taps_x = []
        bias_x = []
        dtb_parts = []
        alog_parts = []
        dskip_parts = []
        taps_shared = jnp.zeros((CONV, 2 * STATE), jnp.float32)
        bias_shared = jnp.zeros((2 * STATE,), jnp.float32)
        grad_bc = jnp.zeros((D, 2 * STATE), jnp.float32)
        normed_gradient = jnp.zeros((LEN, D), jnp.float32)
        for group_idx in range(groups):
            col_lo = group_idx * head_width
            grads = pullbacks[group_idx](d_gated[:, col_lo:col_lo + head_width])
            g_zx, g_bc, g_dt, g_taps, g_bias, g_dtb, g_alog, g_dskip = grads
            zx_parts.append(g_zx)
            dt_parts.append(g_dt)
            bc_rounded_rows = g_bc.astype(jnp.bfloat16)
            grad_bc = grad_bc + jnp.dot(normed.T, bc_rounded_rows, preferred_element_type=jnp.float32)
            normed_gradient = normed_gradient + jnp.dot(bc_rounded_rows, bc_half.T, preferred_element_type=jnp.float32)
            taps_x.append(g_taps[:, :head_width])
            taps_shared = taps_shared + g_taps[:, head_width:]
            bias_x.append(g_bias[:head_width])
            bias_shared = bias_shared + g_bias[head_width:]
            dtb_parts.append(g_dtb)
            alog_parts.append(g_alog)
            dskip_parts.append(g_dskip)
        gate_input_rounded = jnp.concatenate(zx_parts, axis=2).reshape(LEN, 2 * INNER).astype(jnp.bfloat16)
        delta_rounded = jnp.concatenate(dt_parts, axis=1).astype(jnp.bfloat16)
        grad_zx = jnp.dot(normed.T, gate_input_rounded, preferred_element_type=jnp.float32).reshape(D, 2, INNER)
        grad_dt = jnp.dot(normed.T, delta_rounded, preferred_element_type=jnp.float32)
        normed_gradient = normed_gradient + jnp.dot(gate_input_rounded, zx_half.T, preferred_element_type=jnp.float32)
        normed_gradient = normed_gradient + jnp.dot(delta_rounded, dt_half.T, preferred_element_type=jnp.float32)
        weighted_in = input_gain[None, :] * normed_gradient
        grad_ingain = lax.optimization_barrier(jnp.sum(normed_gradient * rows * inv_in, axis=0))
        in_rows = cot_rows + inv_in * weighted_in - rows * inv_in ** 3 * lax.optimization_barrier(jnp.sum(weighted_in * rows, axis=1, keepdims=True)) / D
        grad_taps = jnp.concatenate(taps_x + [taps_shared], axis=1)
        grad_convbias = jnp.concatenate(bias_x + [bias_shared], axis=0)
        terms = (grad_zx, grad_bc, grad_dt, grad_out, grad_ingain, grad_gategain, grad_taps, grad_convbias, jnp.concatenate(dtb_parts), jnp.concatenate(alog_parts), jnp.concatenate(dskip_parts))
        new_totals = tuple((total + term for total, term in zip(totals, terms)))
        return (new_totals, (out_rows, in_rows))
    params = (weight_zx, weight_bc, weight_dt, weight_out, input_gain, gate_gain, conv_taps, conv_bias, dt_bias, a_log, d_skip)
    firsts = (first_zx, first_bc, first_dt, first_out, first_ingain, first_gategain, first_taps, first_convbias, first_dtbias, first_alog, first_dskip)
    seconds = (second_zx, second_bc, second_dt, second_out, second_ingain, second_gategain, second_taps, second_convbias, second_dtbias, second_alog, second_dskip)
    zero_totals = tuple((jnp.zeros(param.shape, jnp.float32) for param in params))
    totals, (block_output, input_grad) = lax.scan(one_sequence, zero_totals, (block_input, cotangent, segments))
    new_params = []
    new_firsts = []
    new_seconds = []
    for index_pos in range(len(params)):
        updated, moment_one, moment_two = adamw_step(params[index_pos], totals[index_pos], firsts[index_pos], seconds[index_pos], index_pos < 4)
        new_params.append(updated)
        new_firsts.append(moment_one)
        new_seconds.append(moment_two)
    return (block_output, input_grad, totals[0], totals[1], totals[2], totals[3], totals[4], totals[5], totals[6], totals[7], totals[8], totals[9], totals[10], new_params[0], new_params[1], new_params[2], new_params[3], new_params[4], new_params[5], new_params[6], new_params[7], new_params[8], new_params[9], new_params[10], new_firsts[0], new_firsts[1], new_firsts[2], new_firsts[3], new_firsts[4], new_firsts[5], new_firsts[6], new_firsts[7], new_firsts[8], new_firsts[9], new_firsts[10], new_seconds[0], new_seconds[1], new_seconds[2], new_seconds[3], new_seconds[4], new_seconds[5], new_seconds[6], new_seconds[7], new_seconds[8], new_seconds[9], new_seconds[10])
```

```python
import functools
import jax
import jax.numpy as jnp
from jax import lax
from jax.experimental import pallas as pl
from jax.experimental.pallas import tpu as pltpu
from jax.sharding import PartitionSpec as P

SPAN = 256
LOG2E = 1.4426950408889634
F32 = jnp.float32
BF = jnp.bfloat16
NN = (((1,), (0,)), ((), ()))
NT = (((1,), (1,)), ((), ()))
TN = (((0,), (0,)), ((), ()))


def dot(a, b, dims=NN, precision=None):
    return lax.dot_general(a, b, dims, precision=precision, preferred_element_type=F32)


def conv_of(x, taps, bias, dpos):
    count = taps.shape[0]
    mixed = bias + taps[count - 1 : count] * x
    for k in range(1, count):
        earlier = jnp.where(dpos >= k, pltpu.roll(x, k, 0), 0.0)
        mixed = mixed + taps[count - 1 - k : count - k] * earlier
    return mixed


def conv_back(x, dm, taps, dpos):
    count = taps.shape[0]
    length = x.shape[0]
    dx = taps[count - 1 : count] * dm
    rows = [jnp.sum(x * dm, axis=0, keepdims=True)]
    for k in range(1, count):
        kept = jnp.where(dpos >= k, dm, 0.0)
        rows.append(jnp.sum(pltpu.roll(x, k, 0) * kept, axis=0, keepdims=True))
        dx = dx + taps[count - 1 - k : count - k] * pltpu.roll(kept, length - k, 0)
    gtaps = jnp.concatenate(rows[::-1], axis=0)
    return dx, gtaps, jnp.sum(dm, axis=0, keepdims=True)


def sig(v):
    return 1.0 / (1.0 + jnp.exp2(v * (-LOG2E)))


def prep_kernel(pbc, dtt, dtb, alog, taps, bias, sege, segr,
                bh, ch, bt, ct, sm, smt, stept, cumt, dpos_out):
    length = pbc.shape[0]
    state = bh.shape[1]
    se = sege[...]
    row = lax.broadcasted_iota(jnp.int32, se.shape, 0)
    dpos = jnp.zeros(se.shape, F32)
    for k in range(1, taps.shape[0]):
        same = (pltpu.roll(se, k, 0) == se) & (row >= k)
        dpos = dpos + jnp.where(same, 1.0, 0.0)
    dpos_out[...] = dpos
    halves = []
    for s in range(2):
        at = slice(s * state, (s + 1) * state)
        mixed = conv_of(pbc[:, at], taps[:, at], bias[:, at], dpos)
        halves.append(mixed * sig(mixed))
    b_act, c_act = halves
    bb, cb = b_act.astype(BF), c_act.astype(BF)
    bh[...] = bb
    ch[...] = cb
    bt[...] = jnp.transpose(b_act).astype(BF)
    ct[...] = jnp.transpose(c_act).astype(BF)
    pre = dtt[...] + dtb[...]
    step = jnp.maximum(pre, 0.0) + jnp.log1p(jnp.exp(-jnp.abs(pre)))
    stept[...] = step
    logd = step * (-jnp.exp(alog[...]) * LOG2E)
    i0 = lax.broadcasted_iota(jnp.int32, (SPAN, SPAN), 0)
    i1 = lax.broadcasted_iota(jnp.int32, (SPAN, SPAN), 1)
    upto = jnp.where(i0 <= i1, 1.0, 0.0)
    for c in range(length // SPAN):
        at = slice(c * SPAN, (c + 1) * SPAN)
        cumt[:, at] = dot(logd[:, at], upto, NN, lax.Precision.HIGHEST)
        scol = jnp.concatenate([se[at]] * (SPAN // se.shape[1]), axis=1)
        same = scol == segr[:, at]
        sm[c] = jnp.where(same & (i0 >= i1), dot(cb[at], bb[at], NT), 0.0)
        smt[c] = jnp.where(same & (i0 <= i1), dot(bb[at], cb[at], NT), 0.0)


def columns(rows, lanes):
    k, length = rows.shape
    each = lanes // k
    wide = jnp.concatenate([jnp.broadcast_to(rows[i : i + 1], (each, length)) for i in range(k)], axis=0)
    return jnp.transpose(wide)


def spread(col, k, each, width):
    return jnp.broadcast_to(col[:, k * each : k * each + 1], (col.shape[0], width))


def fwd_kernel(px, taps, bias, dskip, stept, cumt, bt, ch, sm, sege, dpos, y_out):
    length, lanes = px.shape
    heads = stept.shape[0]
    each = lanes // heads
    lane = lax.broadcasted_iota(jnp.int32, (SPAN, lanes), 1)
    mixed = conv_of(px[...], taps[...], bias[...], dpos[...])
    act = mixed * sig(mixed)
    stepc = columns(stept[...], lanes)
    cumc = columns(cumt[...], lanes)
    xs = act * stepc
    xb = xs.astype(BF)
    ec = jnp.exp2(cumc)
    held = None
    for c in range(length // SPAN):
        at = slice(c * SPAN, (c + 1) * SPAN)
        last = (c + 1) * SPAN - 1
        se = sege[at]
        end = sege[last : last + 1]
        cc = cumc[at]
        parts = []
        for k in range(heads):
            gap = spread(cc, k, each, SPAN) - cumt[k : k + 1, at]
            w = (jnp.exp2(jnp.minimum(gap, 0.0)) * sm[c]).astype(BF)
            parts.append(dot(w, xb[at]))
        out = parts[-1]
        for k in range(heads - 2, -1, -1):
            out = jnp.where(lane < (k + 1) * each, parts[k], out)
        if held is not None:
            prev = sege[c * SPAN - 1 : c * SPAN]
            fs = jnp.where(se == prev, ec[at], 0.0)
            out = out + fs * dot(ch[at], held.astype(BF))
        y_out[at] = out + dskip[...] * act[at]
        if last + 1 < length:
            te = jnp.where(se == end, jnp.exp2(cumc[last : last + 1] - cc), 0.0)
            new = dot(bt[:, at], (te * xs[at]).astype(BF))
            if held is not None:
                keep = jnp.where(end == prev, ec[last : last + 1], 0.0)
                new = new + keep * held
            held = new


def bwd_kernel(px, y, dyb, taps, bias, dskip, stept, cumt, bh, ch, bt, ct, smt, sege, dpos,
               dpx, dst, dbc, dcum, dstep, gtaps, gbias, gskip, glast):
    length, lanes = px.shape
    heads = stept.shape[0]
    state = bh.shape[1]
    each = lanes // heads
    chunks = length // SPAN
    lane = lax.broadcasted_iota(jnp.int32, (SPAN, lanes), 1)

    @pl.when(pl.program_id(0) == 0)
    def _():
        dst[...] = jnp.zeros(dst.shape, F32)
        dbc[...] = jnp.zeros(dbc.shape, F32)

    x = px[...]
    mixed = conv_of(x, taps[...], bias[...], dpos[...])
    s = sig(mixed)
    act = mixed * s
    stepc = columns(stept[...], lanes)
    cumc = columns(cumt[...], lanes)
    xs = act * stepc
    xb = xs.astype(BF)
    ec = jnp.exp2(cumc)
    tos, fss, keeps, enter, txs = [], [], [], [None], []
    for c in range(chunks):
        at = slice(c * SPAN, (c + 1) * SPAN)
        last = (c + 1) * SPAN - 1
        end = sege[last : last + 1]
        te = jnp.where(sege[at] == end, jnp.exp2(cumc[last : last + 1] - cumc[at]), 0.0)
        tos.append(te)
        txs.append((te * xs[at]).astype(BF))
        if c:
            prev = sege[c * SPAN - 1 : c * SPAN]
            fss.append(jnp.where(sege[at] == prev, ec[at], 0.0))
            keeps.append(jnp.where(end == prev, ec[last : last + 1], 0.0))
        else:
            fss.append(None)
            keeps.append(None)
        if c < chunks - 1:
            new = dot(bt[:, at], txs[c])
            if c:
                new = new + keeps[c] * enter[c]
            enter.append(new)
    grad = None
    dxs_parts, used_parts, last_rows = [None] * chunks, [None] * chunks, [None] * chunks
    for c in range(chunks - 1, -1, -1):
        at = slice(c * SPAN, (c + 1) * SPAN)
        dyc = dyb[at]
        dyf = dyc.astype(F32)
        cc = cumc[at]
        parts, total = [], None
        for k in range(heads):
            gap = cumt[k : k + 1, at] - spread(cc, k, each, SPAN)
            d = jnp.exp2(jnp.minimum(gap, 0.0))
            parts.append(dot((d * smt[c]).astype(BF), dyc))
            mine = (lane >= k * each) & (lane < (k + 1) * each)
            term = dot(jnp.where(mine, xb[at], jnp.zeros((), BF)), dyc, NT) * d
            total = term if total is None else total + term
        dst[c] += total
        dxs = parts[-1]
        for k in range(heads - 2, -1, -1):
            dxs = jnp.where(lane < (k + 1) * each, parts[k], dxs)
        used = xb[at].astype(F32) * dxs
        last_rows[c] = jnp.zeros((1, lanes), F32)
        if grad is not None:
            gb = grad.astype(BF)
            back = dot(bh[at], gb)
            ends = txs[c].astype(F32) * back
            dxs = dxs + tos[c] * back
            used = used + ends
            dbc[at, :state] += dot(txs[c], gb, NT)
            last_rows[c] = jnp.sum(ends, axis=0, keepdims=True)
            if c:
                last_rows[c] += jnp.sum(keeps[c] * enter[c] * grad, axis=0, keepdims=True)
        dxs_parts[c] = dxs
        used_parts[c] = used
        if c:
            fdy = (fss[c] * dyf).astype(BF)
            dbc[at, state:] += dot(fdy, enter[c].astype(BF), NT)
            new = dot(ct[:, at], fdy)
            if grad is not None:
                new = new + keeps[c] * grad
            grad = new
    dxs = jnp.concatenate(dxs_parts, axis=0)
    dyf = dyb[...].astype(F32)
    glast[...] = jnp.concatenate(last_rows, axis=0)
    u = dyf * (y[...] - dskip[...] * act) - jnp.concatenate(used_parts, axis=0)
    ut = jnp.transpose(u)
    vt = jnp.transpose(dxs * act)
    dcum[...] = jnp.concatenate([jnp.sum(ut[k * each : (k + 1) * each], axis=0, keepdims=True) for k in range(heads)], axis=0)
    dstep[...] = jnp.concatenate([jnp.sum(vt[k * each : (k + 1) * each], axis=0, keepdims=True) for k in range(heads)], axis=0)
    gskip[...] = jnp.sum(dyf * act, axis=0, keepdims=True)
    dact = dxs * stepc + dskip[...] * dyf
    dm = dact * (s * (1.0 + mixed * (1.0 - s)))
    dx, gt, gb = conv_back(x, dm, taps[...], dpos[...])
    dpx[...] = dx.astype(BF)
    gtaps[...] = gt
    gbias[...] = gb


def post_kernel(pbc, dtt, dtb, alog, taps, bias, sege, segr, dpos, bh, ch, dst, dbc, stept, dcum, dstep, glast,
                dpbc, gtaps, gbias, ddt, gdtb, galog):
    length = pbc.shape[0]
    state = bh.shape[1]
    chunks = length // SPAN
    i0 = lax.broadcasted_iota(jnp.int32, (SPAN, SPAN), 0)
    i1 = lax.broadcasted_iota(jnp.int32, (SPAN, SPAN), 1)
    se = sege[...]
    db, dc = [], []
    for c in range(chunks):
        at = slice(c * SPAN, (c + 1) * SPAN)
        scol = jnp.concatenate([se[at]] * (SPAN // se.shape[1]), axis=1)
        g = jnp.where((scol == segr[:, at]) & (i0 <= i1), dst[c], 0.0)
        db.append(dbc[at, :state] + dot(g.astype(BF), ch[at]))
        dc.append(dbc[at, state:] + dot(jnp.transpose(g).astype(BF), bh[at]))
    for n, parts in enumerate((db, dc)):
        at = slice(n * state, (n + 1) * state)
        x = pbc[:, at]
        mixed = conv_of(x, taps[:, at], bias[:, at], dpos[...])
        s = sig(mixed)
        dm = jnp.concatenate(parts, axis=0) * (s * (1.0 + mixed * (1.0 - s)))
        dx, gt, gb = conv_back(x, dm, taps[:, at], dpos[...])
        dpbc[:, at] = dx.astype(BF)
        gtaps[:, at] = gt
        gbias[:, at] = gb
    rate = -jnp.exp(alog[...])
    back = jnp.where(i0 >= i1, 1.0, 0.0)
    pre = dtt[...] + dtb[...]
    dlogs = []
    for c in range(chunks):
        at = slice(c * SPAN, (c + 1) * SPAN)
        dlogs.append(dot(dcum[:, at], back, NN, lax.Precision.HIGHEST) + glast[:, c : c + 1])
    dlog = jnp.concatenate(dlogs, axis=1)
    galog[...] = jnp.sum(dlog * stept[...] * rate, axis=1, keepdims=True)
    dd = (dstep[...] + dlog * rate) * sig(pre)
    ddt[...] = dd
    gdtb[...] = jnp.sum(dd, axis=1, keepdims=True)


def whole(shape):
    return pl.BlockSpec(shape, lambda *_: (0,) * len(shape))


def params(**kw):
    return pltpu.CompilerParams(vmem_limit_bytes=60 * 1024 * 1024, **kw)


def shape_of(shape, dtype=F32):
    return jax.ShapeDtypeStruct(shape, dtype)


def prep(pbc, dtt, dtb, alog, taps, bias, sege, segr):
    length, two = pbc.shape
    state, heads, chunks = two // 2, dtt.shape[0], length // SPAN
    outs = [shape_of((length, state), BF)] * 2 + [shape_of((state, length), BF)] * 2
    outs += [shape_of((chunks, SPAN, SPAN))] * 2 + [shape_of((heads, length))] * 2 + [shape_of(sege.shape)]
    return pl.pallas_call(prep_kernel, out_shape=outs, name="prep", compiler_params=params())(
        pbc, dtt, dtb, alog, taps, bias, sege, segr)


def pair_spec(rows, lanes, start):
    return pl.BlockSpec((rows, lanes), lambda i: (0, start + i))


def head_spec(heads, length, start):
    return pl.BlockSpec((None, heads, length), lambda i: (start + i, 0, 0))


def mixer_fwd(px, taps, bias, dskip, stept, cumt, bt, ch, sm, sege, dpos, start, count):
    length = px.shape[0]
    lanes = sege.shape[1]
    _, heads, _ = stept.shape
    state = ch.shape[1]
    ins = [pair_spec(length, lanes, start), pair_spec(taps.shape[0], lanes, start), pair_spec(1, lanes, start), pair_spec(1, lanes, start),
           head_spec(heads, length, start), head_spec(heads, length, start),
           whole(bt.shape), whole(ch.shape), whole(sm.shape), whole(sege.shape), whole(dpos.shape)]
    return pl.pallas_call(
        fwd_kernel, out_shape=shape_of((length, lanes * count)), grid=(count,), in_specs=ins,
        out_specs=pl.BlockSpec((length, lanes), lambda i: (0, i)), name="mixfwd", compiler_params=params(),
        cost_estimate=pl.CostEstimate(flops=count * 4_000_000_000, transcendentals=0, bytes_accessed=count * 2_000_000),
    )(px, taps, bias, dskip, stept, cumt, bt, ch, sm, sege, dpos)


def mixer_bwd(px, y, dyb, taps, bias, dskip, stept, cumt, bh, ch, bt, ct, smt, sege, dpos, start, count):
    length = px.shape[0]
    lanes = sege.shape[1]
    _, heads, _ = stept.shape
    ins = [pair_spec(length, lanes, start)] * 3 + [pair_spec(taps.shape[0], lanes, start), pair_spec(1, lanes, start), pair_spec(1, lanes, start),
           head_spec(heads, length, start), head_spec(heads, length, start)]
    ins += [whole(a.shape) for a in (bh, ch, bt, ct, smt, sege, dpos)]
    chunks = length // SPAN
    outs = [
        (shape_of((length, lanes * count), BF), pair_spec(length, lanes, 0)),
        (shape_of(smt.shape), whole(smt.shape)),
        (shape_of((length, 2 * bh.shape[1])), whole((length, 2 * bh.shape[1]))),
        (shape_of((count, heads, length)), head_spec(heads, length, 0)),
        (shape_of((count, heads, length)), head_spec(heads, length, 0)),
        (shape_of((taps.shape[0], lanes * count)), pair_spec(taps.shape[0], lanes, 0)),
        (shape_of((1, lanes * count)), pair_spec(1, lanes, 0)),
        (shape_of((1, lanes * count)), pair_spec(1, lanes, 0)),
        (shape_of((chunks, lanes * count)), pair_spec(chunks, lanes, 0)),
    ]
    return pl.pallas_call(
        bwd_kernel, out_shape=[o[0] for o in outs], grid=(count,), in_specs=ins, out_specs=[o[1] for o in outs],
        name="mixbwd", compiler_params=params(),
        cost_estimate=pl.CostEstimate(flops=count * 8_000_000_000, transcendentals=0, bytes_accessed=count * 4_000_000),
    )(px, y, dyb, taps, bias, dskip, stept, cumt, bh, ch, bt, ct, smt, sege, dpos)


def post(*args):
    pbc, dtt, taps = args[0], args[1], args[4]
    heads = dtt.shape[0]
    outs = [shape_of(pbc.shape, BF), shape_of(taps.shape), shape_of((1, taps.shape[1])), shape_of(dtt.shape), shape_of((heads, 1)), shape_of((heads, 1))]
    return pl.pallas_call(post_kernel, out_shape=outs, name="post", compiler_params=params())(*args)


norm_eps = 1e-05
learn_rate = 0.01
beta_one = 0.9
beta_two = 0.95
adam_eps = 1e-08
weight_decay = 0.1
STEP = 3
TILE = 128


def adamw_step(weight, grad, first, second, decayed):
    new_first = beta_one * first + (1.0 - beta_one) * grad
    new_second = beta_two * second + (1.0 - beta_two) * grad * grad
    first_corr = 1.0 - beta_one**STEP
    second_corr = 1.0 - beta_two**STEP
    update = new_first / first_corr / (jnp.sqrt(new_second / second_corr) + adam_eps)
    if decayed:
        update = update + weight_decay * weight
    return (weight - learn_rate * update, new_first, new_second)


def swap_t(x):
    return lax.ppermute(x, "tensor", [(0, 1), (1, 0)])


def swap_dp(x, b, n):
    return lax.ppermute(x, "dp", [(i, i ^ (1 << b)) for i in range(n)])


def pick(x, i, axis):
    return lax.dynamic_index_in_dim(x, i, axis, keepdims=False)


def merge(mine, got, flag, axis):
    low = jnp.where(flag == 0, mine, got)
    high = jnp.where(flag == 0, got, mine)
    return jnp.stack([low, high], axis=axis)


def join(mine, got, flag, axis):
    low = jnp.where(flag == 0, mine, got)
    high = jnp.where(flag == 0, got, mine)
    return jnp.concatenate([low, high], axis=axis)


class Grid:
    def __init__(self, n):
        self.n = n
        self.count = n.bit_length() - 1
        assert n == 1 << self.count
        self.tp = min(2, self.count - 1)
        self.data = [b for b in range(self.count - 1, -1, -1) if b != self.tp]
        me = lax.axis_index("dp")
        self.flag = [(me >> b) & 1 for b in range(self.count)]

    def swap(self, x, b):
        return swap_dp(x, b, self.n)

    def orders(self):
        d = self.data
        return d, d[:-2] + d[-2:][::-1]

    def gather(self, cur, order):
        have = [self.tp]
        for b in order:
            got = self.swap(cur, b)
            have = sorted(have + [b], reverse=True)
            cur = merge(cur, got, self.flag[b], have.index(b))
        return cur.reshape(-1, cur.shape[-1])

    def scatter(self, full, order):
        have = list(range(self.count - 1, -1, -1))
        x = full.reshape((2,) * self.count + (-1, full.shape[-1]))
        for b in order[::-1]:
            at = have.index(b)
            got = self.swap(pick(x, 1 - self.flag[b], at).astype(BF), b)
            x = pick(x, self.flag[b], at) + got.astype(F32)
            have.remove(b)
        return x


def per_device(n_dp,
    block_input, cotangent, segments, weight_zx, weight_bc, weight_dt, weight_out,
    input_gain, gate_gain, conv_taps, conv_bias, dt_bias, a_log, d_skip, *moments,
):
    firsts, seconds = moments[:11], moments[11:]
    grid = Grid(n_dp)
    order_a, order_b = grid.orders()
    t = lax.axis_index("tensor")
    z = grid.flag[grid.tp]
    rows, _, half = weight_zx.shape
    quarter = half // 2
    model = block_input.shape[2]
    part = block_input.shape[1]
    length = segments.shape[1]
    inner = gate_gain.shape[0]
    heads = weight_dt.shape[1] // 2
    size = quarter // heads
    shared = weight_bc.shape[1]
    state = shared // 2
    taps_n = conv_taps.shape[0]
    col0 = t * half + z * quarter
    head0 = t * heads * 2 + z * heads

    def quarter_of(w, which, width):
        return lax.dynamic_slice_in_dim(w, which * width, width, 1)

    w_x = weight_zx[:, 1].astype(BF)
    w_z = weight_zx[:, 0].astype(BF)
    w_o = jnp.transpose(weight_out).astype(BF)
    w_dt = weight_dt.astype(BF)
    bc_half = weight_bc.astype(BF)
    bc_mine = lax.dynamic_slice_in_dim(bc_half, t * state, state, 1)
    bc_got = swap_t(lax.dynamic_slice_in_dim(bc_half, (1 - t) * state, state, 1))
    bc_rows = join(bc_mine, bc_got, t, 0)

    def pack_x(which):
        dt_part = jnp.pad(quarter_of(w_dt, which, heads), ((0, 0), (0, TILE - heads)))
        return jnp.concatenate([quarter_of(w_x, which, quarter), bc_rows, dt_part], axis=1)

    def paired(make):
        return merge(make(z), grid.swap(make(1 - z), grid.tp), z, 0)

    x2 = block_input[0]
    inv_in = lax.rsqrt(jnp.mean(x2 * x2, axis=1, keepdims=True) + norm_eps)
    normed_part = (x2 * inv_in * input_gain[None, :]).astype(BF)

    cur_x = paired(pack_x)
    split = cur_x.shape[2] // 2
    full_x = jnp.concatenate([grid.gather(cur_x[:, :, :split], order_a), grid.gather(cur_x[:, :, split:], order_b)], axis=1)
    far_part = grid.swap(normed_part, grid.tp)
    normed = [join(p, swap_t(p), t, 0) for p in (normed_part, far_part)]
    full_z = grid.gather(paired(lambda k: quarter_of(w_z, k, quarter)), order_b)
    full_o = grid.gather(paired(lambda k: quarter_of(w_o, k, quarter)), order_a)
    cot_part = cotangent[0].astype(BF)
    cot_far = grid.swap(cot_part, grid.tp)
    cot = [join(p, swap_t(p), t, 0) for p in (cot_part, cot_far)]
    segs = [segments[0], grid.swap(segments, grid.tp)[0]]

    wx = full_x[:, :quarter]
    wbc_half = full_x[:, quarter : quarter + state]
    wbc = join(wbc_half, swap_t(wbc_half), t, 1)
    wdt = full_x[:, quarter + state : quarter + state + heads]

    taps = lax.dynamic_slice_in_dim(conv_taps, col0, quarter, 1)
    bias = lax.dynamic_slice_in_dim(conv_bias, col0, quarter, 0)[None]
    taps_bc, bias_bc = conv_taps[:, inner:], conv_bias[None, inner:]
    dtb = lax.dynamic_slice_in_dim(dt_bias, head0, heads, 0)[:, None]
    alog = lax.dynamic_slice_in_dim(a_log, head0, heads, 0)[:, None]
    dskip = jnp.repeat(lax.dynamic_slice_in_dim(d_skip, head0, heads, 0), size)[None]
    gain = lax.dynamic_slice_in_dim(gate_gain, col0, quarter, 0)[None]
    pairs = quarter // TILE

    fwd = []
    for s in range(2):
        px = dot(normed[s], wx)
        pbc = dot(normed[s], wbc)
        dtt = dot(wdt, normed[s], (((0,), (1,)), ((), ())))
        segf = segs[s].astype(F32)
        sege = jnp.broadcast_to(segf[:, None], (length, TILE))
        segr = segf[None]
        bh, ch, bt, ct, sm, smt, stept, cumt, dpos = prep(pbc, dtt, dtb, alog, taps_bc, bias_bc, sege, segr)
        st3 = stept.reshape(pairs, -1, length)
        cu3 = cumt.reshape(pairs, -1, length)
        y = mixer_fwd(px, taps, bias, dskip, st3, cu3, bt, ch, sm, sege, dpos, 0, pairs)
        fwd.append((px, pbc, dtt, sege, segr, bh, ch, bt, ct, smt, stept, st3, cu3, dpos, y))

    def over_group(v):
        v = v + swap_t(v)
        return v + grid.swap(v, grid.tp)[::-1]

    zs = [dot(normed[s], full_z) for s in range(2)]
    sigs = [jax.nn.sigmoid(v) for v in zs]
    gated = [fwd[s][-1] * (zs[s] * sigs[s]) for s in range(2)]
    sums = over_group(jnp.stack([jnp.sum(g * g, axis=1) for g in gated]))
    inv_gate = lax.rsqrt(sums / inner + norm_eps)[..., None]
    gnorm = [(gated[s] * inv_gate[s] * gain).astype(BF) for s in range(2)]
    grad_o = dot(cot[0], gnorm[0], TN) + dot(cot[1], gnorm[1], TN)

    def to_owner(own, other):
        def over_t(v):
            v = v.reshape(2, part, model)
            return pick(v, t, 0) + swap_t(pick(v, 1 - t, 0).astype(BF)).astype(F32)
        far = grid.swap(over_t(other).astype(BF), grid.tp)
        return over_t(own) + far.astype(F32)

    d_gate = [dot(cot[s], full_o) for s in range(2)]
    cross = over_group(jnp.stack([jnp.sum(d_gate[s] * gain * gated[s], axis=1) for s in range(2)]))[..., None]
    g_gain = sum(jnp.sum(d_gate[s] * gated[s] * inv_gate[s], axis=0) for s in range(2))
    dys, dzs = [], []
    for s in range(2):
        d_gated = inv_gate[s] * gain * d_gate[s] - gated[s] * inv_gate[s] ** 3 * cross[s] / inner
        dys.append((d_gated * (zs[s] * sigs[s])).astype(BF))
        dzs.append((d_gated * fwd[s][-1] * (sigs[s] * (1.0 + zs[s] * (1.0 - sigs[s])))).astype(BF))
    grad_z = dot(normed[0], dzs[0], TN) + dot(normed[1], dzs[1], TN)
    branch = [dot(gnorm[s], full_o, NT) for s in range(2)]

    back = [None, None]
    for s in (1, 0):
        px, pbc, dtt, sege, segr, bh, ch, bt, ct, smt, stept, st3, cu3, dpos, y = fwd[s]
        dpx, dst, dbc, dcum, dstep, gt, gb, gs, gl = mixer_bwd(
            px, y, dys[s], taps, bias, dskip, st3, cu3, bh, ch, bt, ct, smt, sege, dpos, 0, pairs)
        glast = gl.reshape(gl.shape[0], heads, size).sum(-1).T
        dpbc, gtb, gbb, ddt, gdtb, galog = post(
            pbc, dtt, dtb, alog, taps_bc, bias_bc, sege, segr, dpos, bh, ch, dst, dbc, stept,
            dcum.reshape(heads, length), dstep.reshape(heads, length), glast)
        ddt = ddt.astype(BF)
        dn = dot(dzs[s], full_z, NT) + dot(dpx, wx, NT) + dot(dpbc, wbc, NT)
        dn = dn + dot(ddt, wdt, (((0,), (1,)), ((), ())))
        ing = jnp.sum(dn * normed[s].astype(F32), axis=0)
        back[s] = (dpx, dpbc, ddt, dn, ing, gt, gb, gs, gtb, gbb, gdtb, galog)
    own, other = back
    grad_x = dot(normed[0], own[0], TN) + dot(normed[1], other[0], TN)
    grad_b = dot(normed[0], own[1], TN) + dot(normed[1], other[1], TN)
    grad_d = dot(normed[0], own[2], (((0,), (1,)), ((), ()))) + dot(normed[1], other[2], (((0,), (1,)), ((), ())))
    grad_b = pick(grad_b.reshape(model, 2, state), t, 1) + swap_t(pick(grad_b.reshape(model, 2, state), 1 - t, 1).astype(BF)).astype(F32)

    def unpaired(x):
        got = grid.swap(pick(x, 1 - z, 0).astype(BF), grid.tp).astype(F32)
        return pick(x, z, 0), got

    sum_o = join(*unpaired(grid.scatter(grad_o, order_a)), z, 1)
    sum_z = join(*unpaired(grid.scatter(grad_z, order_b)), z, 1)
    grad_xbd = jnp.concatenate([grad_x, grad_b, jnp.pad(grad_d, ((0, 0), (0, TILE - heads)))], axis=1)
    kept = jnp.concatenate([grid.scatter(grad_xbd[:, :split], order_a), grid.scatter(grad_xbd[:, split:], order_b)], axis=2)
    kept, got = unpaired(kept)
    sum_x = join(kept[:, :quarter], got[:, :quarter], z, 1)
    sum_b = kept[:, quarter : quarter + state] + got[:, quarter : quarter + state]
    sum_d = join(kept[:, quarter + state : quarter + state + heads], got[:, quarter + state : quarter + state + heads], z, 1)
    sum_b = sum_b.reshape(2, rows // 2, state)
    grad_bc = join(pick(sum_b, t, 0), swap_t(pick(sum_b, 1 - t, 0)), t, 1)
    grad_zx = jnp.stack([sum_z, sum_x], axis=1)
    grad_out = jnp.transpose(sum_o)

    chan = jnp.concatenate([g_gain[None], own[5] + other[5], own[6] + other[6]], axis=0)
    gskip = (own[7] + other[7]).reshape(heads, size).sum(-1)
    head = jnp.stack([own[10][:, 0] + other[10][:, 0], own[11][:, 0] + other[11][:, 0], gskip])
    head = jnp.pad(head.reshape(-1), (0, TILE - 3 * heads))
    common = jnp.concatenate([(own[8] + other[8]).reshape(-1), (own[9] + other[9]).reshape(-1), (own[4] + other[4]) / input_gain])
    vec = jnp.concatenate([chan.reshape(-1), head, common])
    for b in grid.data:
        vec = vec + grid.swap(vec, b)
    local = vec[: chan.size + TILE]
    common = vec[chan.size + TILE :]
    local = merge(local, grid.swap(local, grid.tp), z, 0)
    common = common + grid.swap(common, grid.tp)
    local = merge(local, swap_t(local), t, 0)
    common = common + swap_t(common)
    chan = jnp.moveaxis(local[:, :, : chan.size].reshape(2, 2, taps_n + 2, quarter), 2, 0).reshape(taps_n + 2, inner)
    head = jnp.moveaxis(local[:, :, chan.size // 4 : chan.size // 4 + 3 * heads].reshape(2, 2, 3, heads), 2, 0).reshape(3, -1)
    tail = common[: (taps_n + 1) * shared].reshape(taps_n + 1, shared)
    grad_gategain = chan[0]
    grad_taps = jnp.concatenate([chan[1 : 1 + taps_n], tail[:taps_n]], axis=1)
    grad_convbias = jnp.concatenate([chan[1 + taps_n], tail[taps_n]])
    grad_dtbias, grad_alog, grad_dskip = head
    grad_ingain = common[(taps_n + 1) * shared :]

    block_output = block_input + to_owner(branch[0], branch[1])[None]
    d_mine = to_owner(own[3], other[3])
    weighted_in = input_gain[None, :] * d_mine
    input_grad = (
        cotangent[0] + inv_in * weighted_in
        - x2 * inv_in**3 * jnp.sum(weighted_in * x2, axis=1, keepdims=True) / model
    )[None]

    weights = (weight_zx, weight_bc, weight_dt, weight_out, input_gain, gate_gain, conv_taps, conv_bias, dt_bias, a_log, d_skip)
    grads = (grad_zx, grad_bc, sum_d, grad_out, grad_ingain, grad_gategain, grad_taps, grad_convbias, grad_dtbias, grad_alog, grad_dskip)
    steps = [adamw_step(weights[i], grads[i], firsts[i], seconds[i], i < 4) for i in range(len(weights))]
    return (block_output, input_grad, *grads, *[s[0] for s in steps], *[s[1] for s in steps], *[s[2] for s in steps])


def solution(mesh):
    big = (P("dp", None, "tensor"), P(("dp", "tensor"), None), P("dp", "tensor"), P("tensor", "dp"))
    small = (P(),) * 7
    tokens = (P("dp", "tensor", None), P("dp", "tensor", None))
    per = big + small
    return jax.shard_map(
        functools.partial(per_device, mesh.shape["dp"]),
        mesh=mesh,
        in_specs=(*tokens, P("dp", None), *per, *per, *per),
        out_specs=(*tokens, *per, *per, *per, *per),
        check_vma=False,
    )
```
